512 devices in a mesh: ctx: 16 (over z_lo, x, core), exp: 32 (over z_hi, y).
Axes of the slice: x: 4, y: 8, z: 8 (z_hi: 4, z_lo: 2; z = z_hi * 2 + z_lo), core: 2. Of those that a mesh axis runs over, the one named last changes fastest.
Arguments:
- frames_in: bfloat16 [16384, 1536], P(('ctx', 'exp')), may hold values from -6 to 6
- expert_ids: int32 [16384, 2], P(('ctx', 'exp')), may hold values from 0 to 31, all different within a row; in each aligned block of 32 rows (0 to 31, 32 to 63, ...) at most 3 rows name the same one
- gate_values: bfloat16 [16384, 2], P(('ctx', 'exp')), may hold values from 0.19921875 to 1
- norm_gain: float32 [1536], replicated, may hold values from 0.1 to 1.9
- weight_in: bfloat16 [32, 1536, 6144], P('exp', None, 'ctx'), may hold values from -0.15625 to 0.15625
- weight_out: bfloat16 [32, 6144, 1536], P('exp', 'ctx'), may hold values from -0.078125 to 0.078125
Outputs:
- mixed: bfloat16 [16384, 1536], P(('ctx', 'exp'))
The draws below stay inside these ranges and needn't reach their ends.
Inputs may be any that keep to these rules, and one draw needn't show every extreme that they name: `expert_ids`: the 2 ids of a frame differ. Among the 32 frames of one device (aligned blocks of frames in order) no expert is named more than 3 times, and that count is reached.
All inputs are finite; a program needn't handle non-finite values.
Results may differ from the reference program's by a relative error of at most 0.007.
Values may be sent and summed in bfloat16 or wider, within the bound.
A program may use at most 64 MiB of HBM per device.

```python
import math
import jax
import jax.numpy as jnp
import numpy as np
from jax import lax

D = 1536
HID = 6144
TOP = 2
FR_DEV = 32
EXPERTS = 32
CAP = 3
FRAMES = 16384
N_CTX = 16
DEVICES = 512


def block_scale(rng, extent, split, smallest, high):
    level = 1.0
    for axis_at, parts in split:
        steps = jax.random.uniform(jax.random.fold_in(jax.random.fold_in(rng, 6), axis_at), (parts,), jnp.float32, smallest / len(split), high / len(split))
        level = level * jnp.repeat(jnp.exp(steps), extent[axis_at] // parts).reshape((-1,) + (1,) * (len(extent) - 1 - axis_at))
    return level


def deal_out(rng, own, number, rows, number_of, top, most, slope):
    ranking = jax.random.permutation(rng, number_of)
    crowded, ordinary = load_shares(number_of, rows * top, most, slope, True), load_shares(number_of, rows * top, most, slope, False)
    places = jnp.arange(number_of)

    def named(tallies, rotation):
        used = int((tallies > 0).sum())
        fixed = max(1, used // 4)
        moved = fixed + (places - fixed + rotation * (used - fixed)) % max(1, number_of - fixed)
        return jnp.zeros((number_of,), jnp.int32).at[ranking[jnp.where(places < fixed, places, moved)]].set(jnp.asarray(tallies, jnp.int32))

    tallies = jnp.where(number % 4 == 0, named(crowded, number // 4), named(ordinary, number - number // 4 - 1))
    mixed = jax.random.permutation(jax.random.fold_in(own, 3), number_of)
    donor, sink = mixed[0:number_of // 2 * 2:2], mixed[1:number_of // 2 * 2:2]
    margin = jnp.minimum(tallies[donor] - 1, most - tallies[sink]) // 2
    margin = jnp.where((donor == ranking[0]) | (sink == ranking[0]) | (tallies[sink] == 0), 0, jnp.maximum(margin, 0))
    moved = jax.random.randint(jax.random.fold_in(own, 4), (number_of // 2,), 0, 1 << 20) % (margin + 1)
    tallies = tallies.at[donor].add(-moved).at[sink].add(moved)
    items = jnp.searchsorted(jnp.cumsum(tallies), jnp.arange(rows * top), side="right").astype(jnp.int32)
    listing = items.reshape(top, rows).T
    listing = listing[jax.random.permutation(jax.random.fold_in(own, 1), rows)]
    rotation = jax.random.randint(jax.random.fold_in(own, 2), (rows, 1), 0, top)
    return jnp.take_along_axis(listing, (jnp.arange(top)[None, :] + rotation) % top, axis=1)


def load_shares(amount, total, bound, lean, full):
    loads = [(1 << 20) // math.isqrt(grade ** lean) + 1 for grade in range(1, amount + 1)]
    largest = bound if full else min(bound, max(-(-total // amount), total * loads[0] // sum(loads)))
    least = 1 if total - largest >= amount - 1 else 0
    given, rest = [largest] + [least] * (amount - 1), total - largest - least * (amount - 1)
    while rest > 0:
        free = [i for i in range(1, amount) if given[i] < largest] or [i for i in range(1, amount) if given[i] < bound]
        pool, remaining = sum([loads[i] for i in free]), rest
        for i in free:
            more = min(bound - given[i], max(1, remaining * loads[i] // pool), rest)
            given[i] = given[i] + more
            rest = rest - more
    return np.array(given)


def scatter_about(rng, dims, scale, bound, shards=(), held_as=jnp.bfloat16):
    entries = jax.random.normal(rng, dims, jnp.float32) * scale
    if len(shards) > 0:
        entries = block_scale(rng, dims, shards, -0.22, 0.18) * entries
    return jnp.clip(entries, min=-bound, max=bound).astype(held_as)


def setup_inputs(seed: int = 0) -> dict:
    streams_of = jax.random.split(jax.random.key(seed), 7)
    frames_in = scatter_about(streams_of[0], (FRAMES, D), 1.0, 6.0, ((0, 512),))
    expert_ids_keys = jax.random.split(jax.random.fold_in(streams_of[1], 1), FRAMES // FR_DEV)
    expert_ids_turns = jax.random.permutation(jax.random.fold_in(streams_of[1], 3), FRAMES // FR_DEV)
    expert_ids = jax.vmap(lambda own, number: deal_out(jax.random.fold_in(streams_of[1], 2), own, number, FR_DEV, EXPERTS, TOP, CAP, 2))(expert_ids_keys, expert_ids_turns).reshape((FRAMES, TOP))
    gate_values = jnp.clip(0.19921875 + 0.80078125 * jax.random.uniform(streams_of[2], (FRAMES, TOP), jnp.float32) ** block_scale(streams_of[2], (FRAMES, TOP), ((0, 512),), -0.2, 0.2), 0.19921875, 1.0).astype(jnp.bfloat16)
    norm_gain = jnp.clip(1.0 + 0.18 * jax.random.normal(streams_of[3], (D,), jnp.float32), 0.1, 1.9)
    weight_in = scatter_about(streams_of[4], (EXPERTS, D, HID), D ** -0.5, 0.15625, ((0, 32), (2, 16)))
    weight_out = scatter_about(streams_of[5], (EXPERTS, HID, D), HID ** -0.5, 0.078125, ((0, 32), (1, 16)))
    return dict(frames_in=frames_in, expert_ids=expert_ids, gate_values=gate_values, norm_gain=norm_gain, weight_in=weight_in, weight_out=weight_out)


EPSILON = 1e-05

def layer_norm(frames, gain):
    values = frames.astype(jnp.float32)
    average = lax.optimization_barrier(jnp.mean(values, axis=-1, keepdims=True))
    centred = values - average
    variance = lax.optimization_barrier(jnp.mean(centred * centred, axis=-1, keepdims=True))
    return (centred * lax.rsqrt(variance + EPSILON) * gain).astype(jnp.bfloat16)

def reference(frames_in, expert_ids, gate_values, norm_gain, weight_in, weight_out):
    normed = layer_norm(frames_in, norm_gain)
    blocks = expert_ids.reshape(DEVICES, FR_DEV * TOP)
    labels = jnp.arange(EXPERTS, dtype=jnp.int32)
    matches = (blocks[:, :, None] == labels[None, None, :]).astype(jnp.int32)
    earlier = jnp.cumsum(matches, axis=1) - matches
    position = lax.optimization_barrier(jnp.sum(matches * earlier, axis=2)).reshape(FRAMES * TOP).astype(jnp.int32)
    flat_ids = expert_ids.reshape(FRAMES * TOP)
    selection = jnp.arange(FRAMES * TOP, dtype=jnp.int32)
    source = selection // (FR_DEV * TOP)
    flat_gates = gate_values.reshape(FRAMES * TOP).astype(jnp.float32)
    slot_count = DEVICES * CAP

    def one_expert(carry, expert):
        target = jnp.where(flat_ids == expert, source * CAP + position, slot_count).astype(jnp.int32)
        picked = jnp.zeros((slot_count,), jnp.int32).at[target].set(selection, mode='drop')
        filled = jnp.zeros((slot_count,), jnp.int32).at[target].set(1, mode='drop')
        frame_rows = jnp.where(filled[:, None] == 1, normed[picked // TOP], jnp.zeros((), jnp.bfloat16))
        hidden = jnp.dot(frame_rows, weight_in[expert], preferred_element_type=jnp.float32)
        activation = (hidden * jax.nn.sigmoid(hidden)).astype(jnp.bfloat16)
        grouped = activation.reshape(slot_count, N_CTX, HID // N_CTX).astype(jnp.float32)
        out_groups = weight_out[expert].reshape(N_CTX, HID // N_CTX, D).astype(jnp.float32)
        partials = jnp.einsum('rch,chd->rcd', grouped, out_groups).astype(jnp.bfloat16)
        summed = lax.optimization_barrier(jnp.sum(partials.astype(jnp.float32), axis=1))
        scaling = filled.astype(jnp.float32) * flat_gates[picked]
        carry = carry.at[picked // TOP].add(summed * scaling[:, None])
        return (carry, None)
    expert_sum, unused = lax.scan(one_expert, jnp.zeros((FRAMES, D), jnp.float32), labels)
    return (frames_in.astype(jnp.float32) + 0.5 * expert_sum).astype(jnp.bfloat16)
```

```python
from functools import partial

import jax
import jax.numpy as jnp
from jax import lax
from jax.sharding import Mesh
from jax.sharding import PartitionSpec as P

CTX = ("ctx_0", "ctx_1", "ctx_2")
CTX_EXP = ("ctx_0", "ctx_1", "ctx_2", "exp")


EPSILON = 1e-05


def exchange_in_groups(x, axis, split_dim, concat_dim, work, item_dim, out_dim):
    items = jax.tree.leaves(x)[0].shape[item_dim]
    count = 2 if items % 2 == 0 else 1
    outs = []
    for k in range(count):
        group = jax.tree.map(
            lambda a: lax.slice_in_dim(
                a, k * (items // count), (k + 1) * (items // count), axis=item_dim
            ),
            x,
        )
        outs.append(
            work(
                lax.all_to_all(
                    group, axis, split_axis=split_dim, concat_axis=concat_dim, tiled=True
                )
            )
        )
    return jax.tree.map(lambda *parts: jnp.concatenate(parts, axis=out_dim), *outs)


def laid_out(pieces, dim):
    dims = list(pieces.shape[1:])
    dims[dim] *= pieces.shape[0]
    return jnp.moveaxis(pieces, 0, dim).reshape(dims)


def gather_in_order(x, axes, order):
    pieces = x
    for k in order:
        pieces = lax.all_gather(pieces, axes[k])
    done = order[::-1]
    back = [done.index(k) for k in range(len(axes))]
    pieces = pieces.transpose(*back, *range(len(axes), pieces.ndim))
    return pieces.reshape(-1, *x.shape)


def whole_of(x, axes, order, dim):
    return laid_out(gather_in_order(x, axes, order), dim)


def in_blocks(x, dim, length):
    before, after = (x.shape[:dim], x.shape[dim + 1 :])
    return jnp.moveaxis(x.reshape(*before, length, -1, *after), dim, 0)


def sent_and_summed(x, axis, dim):
    length = lax.axis_size(axis)
    pieces = lax.all_to_all(in_blocks(x, dim, length), axis, 0, 0, tiled=True)
    return jnp.sum(pieces.astype(jnp.float32), axis=0)


def layer_norm(frames, gain):
    values = frames.astype(jnp.float32)
    average = jnp.mean(values, axis=-1, keepdims=True)
    centred = values - average
    variance = jnp.mean(centred * centred, axis=-1, keepdims=True)
    return (centred * lax.rsqrt(variance + EPSILON) * gain).astype(jnp.bfloat16)


def slot_tables(expert_ids, gate_values, experts, capacity):
    frames, width = expert_ids.shape
    flat_ids = expert_ids.reshape(frames * width)
    labels = jnp.arange(experts, dtype=jnp.int32)
    matches = (flat_ids[:, None] == labels[None, :]).astype(jnp.int32)
    earlier = jnp.cumsum(matches, axis=0) - matches
    position = jnp.sum(matches * earlier, axis=1)
    slot_match = (position[:, None] == jnp.arange(capacity, dtype=jnp.int32)[None, :]).astype(
        jnp.float32
    )
    chosen = (matches.astype(jnp.float32)[:, :, None] * slot_match[:, None, :]).reshape(
        frames, width, experts, capacity
    )
    dispatch = jnp.sum(chosen, axis=1)
    weighing = jnp.sum(chosen * gate_values.astype(jnp.float32)[:, :, None, None], axis=1)
    return (dispatch.astype(jnp.bfloat16), weighing.astype(jnp.bfloat16))


def expert_partial(frame_rows, weight_in, weight_out):
    hidden = jnp.einsum(
        "...d,dh->...h", frame_rows, weight_in[0], preferred_element_type=jnp.float32
    )
    activation = (hidden * jax.nn.sigmoid(hidden)).astype(jnp.bfloat16)
    return jnp.einsum(
        "...h,hd->...d", activation, weight_out[0], preferred_element_type=jnp.float32
    ).astype(jnp.bfloat16)


def local(frames_in, expert_ids, gate_values, norm_gain, weight_in, weight_out):
    experts = lax.axis_size("exp")
    frames, selections = expert_ids.shape
    capacity = max(2, 3 * frames * selections // (2 * experts))
    normed = layer_norm(frames_in, norm_gain)
    dispatch, weighing = slot_tables(expert_ids, gate_values, experts, capacity)
    buffer = jnp.einsum(
        "fes,fd->esd", dispatch, normed, preferred_element_type=jnp.float32
    ).astype(jnp.bfloat16)
    received = lax.all_to_all(buffer, "exp", split_axis=0, concat_axis=0, tiled=True)
    shared = lax.all_gather(received.reshape(experts * capacity, -1), CTX, axis=0, tiled=True)
    partials = expert_partial(shared, weight_in, weight_out)
    summed = lax.psum_scatter(partials, CTX, scatter_dimension=0, tiled=True)
    back = lax.all_to_all(
        summed.reshape(experts, capacity, -1), "exp", split_axis=0, concat_axis=0, tiled=True
    )
    expert_sum = jnp.einsum("fes,esd->fd", weighing, back, preferred_element_type=jnp.float32)
    return (frames_in.astype(jnp.float32) + 0.5 * expert_sum).astype(jnp.bfloat16)


def solution(mesh):
    split = Mesh(
        mesh.devices.reshape(2, 4, 2, mesh.shape["exp"]), ("ctx_0", "ctx_1", "ctx_2", "exp")
    )
    return jax.shard_map(
        local,
        mesh=split,
        in_specs=(
            P(CTX_EXP, None),
            P(CTX_EXP, None),
            P(CTX_EXP, None),
            P(),
            P("exp", None, CTX),
            P("exp", CTX, None),
        ),
        out_specs=P(CTX_EXP, None),
        check_vma=False,
    )
```
